1024 devices in a mesh: dp: 64 (over x, y, core), mp: 16 (over z).
Axes of the slice: x: 4, y: 8, z: 16, core: 2. Of those that a mesh axis runs over, the one named last changes fastest.
Arguments:
- patches: bfloat16 [2048, 81920], P('dp', 'mp'), may hold values from -10 to 10
- norm_gain: float32 [1280], replicated, may hold values from 0.1 to 1.9
- qkv_weight: bfloat16 [1280, 3840], P(None, 'mp'), may hold values from -6 to 6
- out_weight: bfloat16 [1280, 1280], P('mp'), may hold values from -0.15625 to 0.15625
- window_plan: int32 [64, 32], replicated, may hold values from -1 to 63, as said below
Outputs:
- attended: bfloat16 [2048, 81920], P('dp', 'mp')
The draws below stay inside these ranges and needn't reach their ends.
Inputs may be any that keep to these rules, and one draw needn't show every extreme that they name: `window_plan`: each home's live slots come first; over all homes every encoder device is named by exactly 16 slots; one home names one encoder at most 1 times and some home reaches that; the busiest home has all 32 slots live.
All inputs are finite; a program needn't handle non-finite values.
Results may differ from the reference program's by a relative error of at most 0.018.
Values may be sent and summed in bfloat16 or wider, within the bound.
No kernel may reach another device: no remote copies, remote signals or barrier semaphores. Data moves between devices by JAX's collectives and lax.ppermute only.
A program may use at most 128 MiB of HBM per device.

```python
import math
import jax
import jax.numpy as jnp
from jax import lax

D = 1280
HEADS = 16
HEAD_DIM = 80
WIN = 64
ENC_WIN = 16
HOME_WIN = 32
HOMES = 64
WINDOWS = 2048
ROWS = 131072
N_MP = 16


def draw_patches(key, part):
    first_key, second_key, third_key = jax.random.split(jax.random.fold_in(key, 11), 3)
    draws_raw = jnp.clip(jax.random.normal(first_key, (ROWS, D), jnp.float32), -3.0, 3.0)
    row_scale = jnp.exp(jax.random.uniform(second_key, (ROWS, 1), jnp.float32, math.log(0.1), math.log(1.0)))
    col_scale = jnp.exp(jax.random.uniform(third_key, (1, D), jnp.float32, math.log(0.25), math.log(2.5)))
    values = (draws_raw * row_scale * col_scale).reshape(ROWS // WIN, WIN, D)
    return jnp.transpose(values, (0, 2, 1)).reshape(ROWS // WIN, D * WIN).astype(jnp.bfloat16)


def draw_qkv_weight(key, part):
    first_key = jax.random.fold_in(jax.random.fold_in(key, 23), 0)
    weights = jnp.clip(jax.random.normal(first_key, (D, HEADS, 3, HEAD_DIM), jnp.float32), -4.0, 4.0) * D ** (-0.5)
    return weights.reshape(D, 3 * D).astype(jnp.bfloat16)


def draw_window_plan(key, part):
    first_key, second_key, third_key = jax.random.split(jax.random.fold_in(key, 37), 3)
    home_order = jax.random.permutation(first_key, HOMES)
    spread = jax.random.randint(second_key, (HOMES // 2,), 0, ENC_WIN + 1).astype(jnp.int32)
    spread = spread.at[0].set(ENC_WIN)
    paired = jnp.stack([ENC_WIN + spread, ENC_WIN - spread], axis=1).reshape(HOMES)
    counts = jnp.zeros((HOMES,), jnp.int32).at[home_order].set(paired)
    offsets = jnp.cumsum(counts) - counts
    targets = jax.random.permutation(third_key, HOMES).astype(jnp.int32)
    columns = jnp.arange(HOME_WIN, dtype=jnp.int32)
    encoder_of = targets[(offsets[:, None] + columns[None, :]) % HOMES]
    return jnp.where(columns[None, :] < counts[:, None], encoder_of, -1).astype(jnp.int32)


def levels(own_key, extent, cuts, least, largest):
    def one(axis_at, shards_of):
        steps = jax.random.uniform(jax.random.fold_in(jax.random.fold_in(own_key, 6), axis_at), (shards_of,), jnp.float32, least / len(cuts), largest / len(cuts))
        return jnp.repeat(jnp.exp(steps), extent[axis_at] // shards_of).reshape((-1,) + (1,) * (len(extent) - axis_at - 1))

    gain = one(*cuts[0])
    for cut in cuts[1:]:
        gain = gain * one(*cut)
    return gain


def noise(key, dims, deviation, bound, shards=(), kind=jnp.bfloat16):
    array = jax.random.normal(key, dims, jnp.float32) * deviation
    if len(shards) > 0:
        array = levels(key, dims, shards, -0.22, 0.18) * array
    return jnp.clip(array, min=-bound, max=bound).astype(kind)


def setup_inputs(seed: int = 0) -> dict:
    key_of = jax.random.split(jax.random.key(seed), 6)
    patches = draw_patches(jax.random.fold_in(key_of[5], 71), 0)
    norm_gain = jnp.clip(1.0 + 0.18 * jax.random.normal(key_of[1], (D,), jnp.float32), 0.1, 1.9)
    qkv_weight = draw_qkv_weight(jax.random.fold_in(key_of[5], 71), 0)
    out_weight = noise(key_of[3], (D, D), D ** -0.5, 0.15625, ((0, 16),))
    window_plan = draw_window_plan(jax.random.fold_in(key_of[5], 71), 0)
    return dict(patches=patches, norm_gain=norm_gain, qkv_weight=qkv_weight, out_weight=out_weight, window_plan=window_plan)


epsilon = 1e-06

def attend(window_block, norm_gain, qkv_weight, out_weight):
    count = window_block.shape[0]
    as_float = window_block.astype(jnp.float32)
    mean_square = lax.optimization_barrier(jnp.mean(as_float * as_float, axis=-1, keepdims=True))
    normed = (as_float * lax.rsqrt(mean_square + epsilon) * norm_gain).astype(jnp.bfloat16)
    projected = jnp.dot(normed.reshape(count * WIN, D), qkv_weight, preferred_element_type=jnp.float32)
    projected = lax.optimization_barrier(projected.astype(jnp.bfloat16)).astype(jnp.float32)
    projected = projected.reshape(count, WIN, HEADS, 3, HEAD_DIM)
    queries = projected[:, :, :, 0, :]
    key_vecs = projected[:, :, :, 1, :]
    value_vecs = projected[:, :, :, 2, :]
    scores = jnp.einsum('wqhd,wkhd->whqk', queries, key_vecs) * HEAD_DIM ** (-0.5)
    probs = jax.nn.softmax(scores, axis=-1)
    probs = lax.optimization_barrier(probs.astype(jnp.bfloat16)).astype(jnp.float32)
    heads_out = jnp.einsum('whqk,wkhd->wqhd', probs, value_vecs).astype(jnp.bfloat16)
    flat_heads = heads_out.reshape(count * WIN, D)
    group_width = D // N_MP
    summed = jnp.zeros((count * WIN, D), jnp.float32)
    for group in range(N_MP):
        lower = group * group_width
        piece = flat_heads[:, lower:lower + group_width]
        partial_term = jnp.dot(piece, out_weight[lower:lower + group_width, :], preferred_element_type=jnp.float32)
        partial_term = lax.optimization_barrier(partial_term.astype(jnp.bfloat16)).astype(jnp.float32)
        summed = summed + partial_term
    block_out = (as_float + summed.reshape(count, WIN, D)).astype(jnp.bfloat16)
    return block_out

def reference(patches, norm_gain, qkv_weight, out_weight, window_plan):
    blocks = jnp.transpose(patches.reshape(WINDOWS, D, WIN), (0, 2, 1)).reshape(HOMES, HOME_WIN, WIN, D)
    results = lax.map(lambda window_block: attend(window_block, norm_gain, qkv_weight, out_weight), blocks)
    live_mask = (window_plan >= 0)[:, :, None, None]
    results = jnp.where(live_mask, results, jnp.zeros_like(results))
    results = jnp.transpose(results.reshape(WINDOWS, WIN, D), (0, 2, 1))
    return results.reshape(WINDOWS, D * WIN)
```

```python
import jax
import jax.numpy as jnp
from jax import lax
from jax.experimental import pallas as pl
from jax.experimental.pallas import tpu as pltpu
from jax.sharding import Mesh, PartitionSpec as P

HEADS = 16
HEAD_DIM = 80
WIN = 64
WIDTH = 1280
LANES = 128
QKV_ROWS = 3 * HEAD_DIM
HEAD_ROWS = QKV_ROWS + HEAD_DIM
TILE_ROWS = 8
CHUNKS = WIDTH // LANES
PIECES = 64
PIECE_TILES = 7
PIECE_ROWS = PIECE_TILES * TILE_ROWS
SLAB_ROWS = PIECES * PIECE_ROWS
HEAD_STEP = 4
epsilon = 1e-06


def piece_kernel(index_ref, gain_ref, qkv_ref, out_ref, piece_ref):
    tiles_per_chunk = HEAD_ROWS // TILE_ROWS
    for step in range(PIECE_TILES):
        tile = index_ref[0] * PIECE_TILES + step
        tile = jnp.minimum(tile, CHUNKS * tiles_per_chunk - 1)
        chunk = tile // tiles_per_chunk
        row = (tile - chunk * tiles_per_chunk) * TILE_ROWS
        column = pl.multiple_of(chunk * LANES, LANES)
        rows = pl.ds(step * TILE_ROWS, TILE_ROWS)

        @pl.when(row < QKV_ROWS)
        def _():
            block = qkv_ref[pl.ds(pl.multiple_of(row, TILE_ROWS), TILE_ROWS), pl.ds(column, LANES)]
            gain = gain_ref[:, pl.ds(column, LANES)]
            piece_ref[rows, :] = (block.astype(jnp.float32) * gain).astype(jnp.bfloat16)

        @pl.when(row >= QKV_ROWS)
        def _():
            below = pl.multiple_of(row - QKV_ROWS, TILE_ROWS)
            piece_ref[rows, :] = out_ref[pl.ds(below, TILE_ROWS), pl.ds(column, LANES)]


def weight_piece(index, norm_gain, qkv_t, out_weight):
    vmem = pl.BlockSpec(memory_space=pltpu.VMEM)
    return pl.pallas_call(
        piece_kernel,
        out_shape=jax.ShapeDtypeStruct((PIECE_ROWS, LANES), jnp.bfloat16),
        in_specs=[pl.BlockSpec(memory_space=pltpu.SMEM), vmem, vmem, vmem],
        out_specs=vmem,
    )(index, norm_gain, qkv_t, out_weight)


def flat(ref):
    return ref.reshape(SLAB_ROWS, LANES)


def attend_kernel(live_ref, x_ref, *refs):
    slab_refs, (o_ref, out_sc, heads_sc) = refs[:HEAD_STEP], refs[HEAD_STEP:]
    step = pl.program_id(0)
    x = x_ref[...]
    xf = x.astype(jnp.float32)
    scale = lax.rsqrt(jnp.sum(xf * xf, axis=0, keepdims=True) * (1.0 / WIDTH) + epsilon)
    lane = lax.broadcasted_iota(jnp.int32, (WIN, LANES), 1)
    first = lane < WIN
    for local in range(HEAD_STEP):
        slab = flat(slab_refs[local])
        projected = None
        for pair in range(CHUNKS // 2):
            base = 2 * pair * HEAD_ROWS
            weights = jnp.concatenate(
                [slab[base:base + QKV_ROWS, :], slab[base + HEAD_ROWS:base + HEAD_ROWS + QKV_ROWS, :]], axis=1)
            term = jnp.dot(weights, x[2 * pair * LANES:2 * (pair + 1) * LANES, :],
                           preferred_element_type=jnp.float32)
            projected = term if projected is None else projected + term
        projected = (projected * scale).astype(jnp.bfloat16)
        queries = projected[:HEAD_DIM]
        keys = projected[HEAD_DIM:2 * HEAD_DIM]
        values = projected[2 * HEAD_DIM:]
        scores = lax.dot_general(keys, queries, (((0,), (0,)), ((), ())), preferred_element_type=jnp.float32)
        scores = jnp.where(first, scores[:WIN], scores[WIN:]) * HEAD_DIM ** (-0.5)
        scores = jnp.exp(scores - jnp.max(scores, axis=0, keepdims=True))
        probs = scores / jnp.sum(scores, axis=0, keepdims=True)
        zero = jnp.zeros_like(probs)
        probs = jnp.concatenate([jnp.where(first, probs, zero), jnp.where(first, zero, probs)], axis=0)
        out = jnp.dot(values, probs.astype(jnp.bfloat16), preferred_element_type=jnp.float32)
        rows = pl.ds(pl.multiple_of((step * HEAD_STEP + local) * HEAD_DIM, 16), HEAD_DIM)
        heads_sc[rows, :] = out.astype(jnp.bfloat16)
        for chunk in range(CHUNKS):
            base = chunk * HEAD_ROWS + QKV_ROWS
            out_sc[rows, chunk * LANES:(chunk + 1) * LANES] = slab[base:base + HEAD_DIM, :]

    @pl.when(step == pl.num_programs(0) - 1)
    def _():
        partial = lax.dot_general(heads_sc[...], out_sc[...], (((0,), (0,)), ((), ())),
                                  preferred_element_type=jnp.float32)
        total = xf + partial.T
        row_lane = lax.broadcasted_iota(jnp.int32, (1, LANES), 1)
        live = jnp.where(row_lane < WIN, live_ref[0], live_ref[1]) >= 0
        o_ref[...] = jnp.where(live, total, 0.0).astype(jnp.bfloat16)


def attend(live, x, slabs):
    return pl.pallas_call(
        attend_kernel,
        grid=(HEADS // HEAD_STEP,),
        out_shape=jax.ShapeDtypeStruct((WIDTH, LANES), jnp.bfloat16),
        in_specs=[
            pl.BlockSpec(memory_space=pltpu.SMEM),
            pl.BlockSpec((WIDTH, LANES), lambda i: (0, 0)),
        ] + [
            pl.BlockSpec((PIECES, None, PIECE_ROWS, LANES), lambda i, local=local: (0, HEAD_STEP * i + local, 0, 0))
            for local in range(HEAD_STEP)
        ],
        out_specs=pl.BlockSpec((WIDTH, LANES), lambda i: (0, 0)),
        scratch_shapes=[pltpu.VMEM((WIDTH, WIDTH), jnp.bfloat16), pltpu.VMEM((WIDTH, LANES), jnp.bfloat16)],
        compiler_params=pltpu.CompilerParams(vmem_limit_bytes=48 << 20),
    )(live, x, *([slabs] * HEAD_STEP))


def body(patches, norm_gain, qkv_weight, out_weight, window_plan):
    home = (lax.axis_index("x") * 8 + lax.axis_index("y")) * 2 + lax.axis_index("c")
    spot = lax.axis_index("z")
    piece = weight_piece(home.reshape(1).astype(jnp.int32), norm_gain.reshape(1, WIDTH), qkv_weight.T, out_weight)
    slabs = lax.all_gather(piece, ("x", "y", "c", "z"), axis=0, tiled=True)
    slabs = slabs.reshape(PIECES, HEADS, PIECE_ROWS, LANES)
    share = patches.shape[1] // WIN
    pairs = patches.reshape(16, 2, share, WIN).transpose(0, 2, 1, 3).reshape(16, share, LANES)
    mine = lax.all_to_all(pairs, "z", 0, 0, tiled=True).reshape(WIDTH, LANES)
    live = lax.dynamic_slice(window_plan, (home, spot * 2), (1, 2))[0]
    done = attend(live, mine, slabs).reshape(16, share, LANES)
    back = lax.all_to_all(done, "z", 0, 0, tiled=True)
    return back.reshape(16, share, 2, WIN).transpose(0, 2, 1, 3).reshape(32, share * WIN)


def solution(mesh):
    grid = Mesh(mesh.devices.reshape(4, 8, 2, 16), ("x", "y", "c", "z"))
    home = ("x", "y", "c")
    return jax.shard_map(
        body,
        mesh=grid,
        in_specs=(P(home, "z"), P(), P(None, "z"), P("z", None), P()),
        out_specs=P(home, "z"),
        check_vma=False,
    )
```

```python
import jax
import jax.numpy as jnp
from jax import lax
from jax.experimental import pallas as pl
from jax.experimental.pallas import tpu as pltpu
from jax.sharding import Mesh, PartitionSpec as P


HEAD_DIM = 80
WIN = 64
WIDTH = 1280
LANES = 128
QKV_ROWS = 3 * HEAD_DIM
HEAD_ROWS = QKV_ROWS + HEAD_DIM
TILE_ROWS = 8
HALF_CHUNKS = 5
HALF_WIDTH = HALF_CHUNKS * LANES
PIECES = 32
PIECE_TILES = 7
PIECE_ROWS = PIECE_TILES * TILE_ROWS
SLAB_ROWS = PIECES * PIECE_ROWS
HEADS_HERE = 4
HEAD_STEP = 2
MATES = 4
SPAN = MATES * LANES
epsilon = 1e-06


def piece_kernel(index_ref, qkv_ref, out_ref, pieces_ref):
    tiles_per_chunk = HEAD_ROWS // TILE_ROWS
    for which in range(2):
        for step in range(PIECE_TILES):
            tile = jnp.minimum(index_ref[1 + which] * PIECE_TILES + step, HALF_CHUNKS * tiles_per_chunk - 1)
            chunk = tile // tiles_per_chunk
            row = (tile - chunk * tiles_per_chunk) * TILE_ROWS
            column = pl.multiple_of((chunk + index_ref[0] * HALF_CHUNKS) * LANES, LANES)
            rows = slice(step * TILE_ROWS, (step + 1) * TILE_ROWS)

            @pl.when(row < QKV_ROWS)
            def _():
                here = pl.ds(pl.multiple_of(jnp.minimum(row, QKV_ROWS - TILE_ROWS), TILE_ROWS), TILE_ROWS)
                pieces_ref[which, rows, :] = qkv_ref[here, pl.ds(column, LANES)]

            @pl.when(row >= QKV_ROWS)
            def _():
                here = pl.ds(pl.multiple_of(jnp.maximum(row - QKV_ROWS, 0), TILE_ROWS), TILE_ROWS)
                pieces_ref[which, rows, :] = out_ref[here, pl.ds(column, LANES)]


def weight_pieces(index, qkv_t, out_weight):
    vmem = pl.BlockSpec(memory_space=pltpu.VMEM)
    return pl.pallas_call(
        piece_kernel,
        out_shape=jax.ShapeDtypeStruct((2, PIECE_ROWS, LANES), jnp.bfloat16),
        in_specs=[pl.BlockSpec(memory_space=pltpu.SMEM), vmem, vmem],
        out_specs=vmem,
    )(index, qkv_t, out_weight)


def norm_kernel(gain_ref, *refs):
    out_ref = refs[MATES]
    for mate in range(MATES):
        x = refs[mate][...].astype(jnp.float32)
        scale = lax.rsqrt(jnp.sum(x * x, axis=0, keepdims=True) * (1.0 / WIDTH) + epsilon)
        out_ref[:, mate * LANES:(mate + 1) * LANES] = (x * scale * gain_ref[...]).astype(jnp.bfloat16)


def normalize(gain, groups):
    vmem = pl.BlockSpec(memory_space=pltpu.VMEM)
    return pl.pallas_call(
        norm_kernel,
        out_shape=jax.ShapeDtypeStruct((WIDTH, SPAN), jnp.bfloat16),
        in_specs=[vmem] * (1 + MATES),
        out_specs=vmem,
    )(gain, *groups)


def flat(ref):
    return ref.reshape(SLAB_ROWS, LANES)


def attend_kernel(core_ref, x_ref, *refs):
    slab_refs, out_refs, scratch = refs[:2 * HEAD_STEP], refs[2 * HEAD_STEP:-3], refs[-3:]
    proj_sc, heads_sc = scratch[:2], scratch[2]
    step = pl.program_id(0)
    starts = [pl.multiple_of(core_ref[0] * HALF_WIDTH, LANES),
              pl.multiple_of((1 - core_ref[0]) * HALF_WIDTH, LANES)]
    first = lax.broadcasted_iota(jnp.int32, (WIN, LANES), 1) < WIN
    for local in range(HEAD_STEP):
        rows = pl.ds(pl.multiple_of((step * HEAD_STEP + local) * HEAD_DIM, 16), HEAD_DIM)
        projected = None
        for half in range(2):
            slab = flat(slab_refs[2 * local + half])
            bases = [chunk * HEAD_ROWS for chunk in range(HALF_CHUNKS)]
            weights = jnp.concatenate([slab[base:base + QKV_ROWS, :] for base in bases], axis=1)
            term = jnp.dot(weights, x_ref[pl.ds(starts[half], HALF_WIDTH), :], preferred_element_type=jnp.float32)
            projected = term if projected is None else projected + term
            for chunk, base in enumerate(bases):
                proj_sc[half][rows, chunk * LANES:(chunk + 1) * LANES] = slab[base + QKV_ROWS:base + HEAD_ROWS, :]
        projected = projected.astype(jnp.bfloat16)
        for mate in range(MATES):
            span = projected[:, mate * LANES:(mate + 1) * LANES]
            queries, keys, values = span[:HEAD_DIM], span[HEAD_DIM:2 * HEAD_DIM], span[2 * HEAD_DIM:]
            scores = lax.dot_general(keys, queries, (((0,), (0,)), ((), ())), preferred_element_type=jnp.float32)
            scores = jnp.where(first, scores[:WIN], scores[WIN:]) * HEAD_DIM ** (-0.5)
            scores = jnp.exp(scores - jnp.max(scores, axis=0, keepdims=True))
            probs = scores / jnp.sum(scores, axis=0, keepdims=True)
            zero = jnp.zeros_like(probs)
            probs = jnp.concatenate([jnp.where(first, probs, zero), jnp.where(first, zero, probs)], axis=0)
            out = jnp.dot(values, probs.astype(jnp.bfloat16), preferred_element_type=jnp.float32)
            heads_sc[rows, mate * LANES:(mate + 1) * LANES] = out.astype(jnp.bfloat16)

    @pl.when(step == pl.num_programs(0) - 1)
    def _():
        for half in range(2):
            partial = lax.dot_general(proj_sc[half][...], heads_sc[...], (((0,), (0,)), ((), ())),
                                      preferred_element_type=jnp.float32)
            for mate in range(MATES):
                piece = partial[:, mate * LANES:(mate + 1) * LANES]
                out_refs[mate][pl.ds(starts[half], HALF_WIDTH), :] = piece.astype(out_refs[mate].dtype)


def attend(core, x, own, other):
    whole = pl.BlockSpec((WIDTH, LANES), lambda i: (0, 0))
    slabs, specs = [], []
    for local in range(HEAD_STEP):
        for half in (own, other):
            slabs.append(half)
            specs.append(pl.BlockSpec((PIECES // 2, None, 2 * PIECE_ROWS, LANES),
                                      lambda i, local=local: (0, HEAD_STEP * i + local, 0, 0)))
    return pl.pallas_call(
        attend_kernel,
        grid=(HEADS_HERE // HEAD_STEP,),
        out_shape=[jax.ShapeDtypeStruct((WIDTH, LANES), jnp.float32)]
        + [jax.ShapeDtypeStruct((WIDTH, LANES), jnp.bfloat16)] * (MATES - 1),
        in_specs=[pl.BlockSpec(memory_space=pltpu.SMEM), pl.BlockSpec((WIDTH, SPAN), lambda i: (0, 0))] + specs,
        out_specs=[whole] * MATES,
        scratch_shapes=[pltpu.VMEM((HEADS_HERE * HEAD_DIM, HALF_WIDTH), jnp.bfloat16)] * 2
        + [pltpu.VMEM((HEADS_HERE * HEAD_DIM, SPAN), jnp.bfloat16)],
        compiler_params=pltpu.CompilerParams(vmem_limit_bytes=24 << 20),
    )(core, x, *slabs)


def trade(value, axes):
    count = 2 ** len(axes)
    return lax.ppermute(value, axes, [(i, count - 1 - i) for i in range(count)])


def exchange(values):
    across, along, both = values
    return trade(across, ("xb",)), trade(along, ("zp",)), trade(both, ("xb", "zp"))


def body(patches, norm_gain, qkv_weight, out_weight, window_plan):
    index = lax.axis_index
    core = index("c")
    home = ((index("xa") * 2 + index("xb")) * 8 + index("y")) * 2 + core
    spot = index("zh") * 2 + index("zp")
    bit = index("zh") % 2
    place = (index("xa") * 8 + index("y")) * 2
    numbers = jnp.stack([core, place + bit, place + 1 - bit]).astype(jnp.int32)
    pieces = weight_pieces(numbers, qkv_weight.T, out_weight)
    moved = lax.ppermute(pieces[1], "zh", [(i, i ^ 1) for i in range(8)])
    mine_first = jnp.where(bit == index("xb"), pieces[0], moved)
    own = lax.all_gather(mine_first, ("xa", "y", "zh"), axis=0, tiled=True)

    share = patches.shape[1] // WIN
    pairs = patches.reshape(16, 2, share, WIN).transpose(0, 2, 1, 3).reshape(16, share, LANES)
    mine = lax.all_to_all(pairs, ("zh", "zp"), 0, 0, tiled=True).reshape(WIDTH, LANES)
    normed = normalize(norm_gain.reshape(WIDTH, 1), (mine,) + exchange((mine, mine, mine)))
    own, normed = lax.optimization_barrier((own, normed))
    other = lax.ppermute(own, "c", [(0, 1), (1, 0)])
    shape = (PIECES // 2, HEADS_HERE, 2 * PIECE_ROWS, LANES)
    kept, *sent = attend(core.reshape(1).astype(jnp.int32), normed, own.reshape(shape), other.reshape(shape))
    total = mine.astype(jnp.float32) + kept
    for part in exchange(sent):
        total = total + part.astype(jnp.float32)
    live = lax.dynamic_slice(window_plan, (home, spot * 2), (1, 2))[0] >= 0
    total = jnp.where(jnp.repeat(live, WIN)[None, :], total, 0.0)
    done = total.astype(jnp.bfloat16).reshape(16, share, LANES)
    back = lax.all_to_all(done, ("zh", "zp"), 0, 0, tiled=True)
    return back.reshape(16, share, 2, WIN).transpose(0, 2, 1, 3).reshape(32, share * WIN)


def solution(mesh):
    grid = Mesh(mesh.devices.reshape(2, 2, 8, 2, 8, 2), ("xa", "xb", "y", "c", "zh", "zp"))
    home, feature = ("xa", "xb", "y", "c"), ("zh", "zp")
    return jax.shard_map(
        body,
        mesh=grid,
        in_specs=(P(home, feature), P(), P(None, feature), P(feature, None), P()),
        out_specs=P(home, feature),
        check_vma=False,
    )
```

```python
import jax
import jax.numpy as jnp
from jax import lax
from jax.experimental import pallas as pl
from jax.experimental.pallas import tpu as pltpu
from jax.sharding import Mesh, PartitionSpec as P


HEAD_DIM = 80
WIN = 64
WIDTH = 1280
LANES = 128
QKV_ROWS = 3 * HEAD_DIM
HEAD_ROWS = QKV_ROWS + HEAD_DIM
TILE_ROWS = 8
HALF_CHUNKS = 5
HALF_WIDTH = HALF_CHUNKS * LANES
PIECES = 8
PIECE_TILES = 25
PIECE_ROWS = PIECE_TILES * TILE_ROWS
SLAB_ROWS = PIECES * PIECE_ROWS
HEADS_HERE = 4
HEAD_STEP = 2
MATES = 4
SPAN = MATES * LANES
epsilon = 1e-06


def piece_kernel(index_ref, qkv_ref, out_ref, piece_ref):
    tiles_per_chunk = HEAD_ROWS // TILE_ROWS
    for step in range(PIECE_TILES):
        tile = index_ref[1] * PIECE_TILES + step
        chunk = tile // tiles_per_chunk
        row = (tile - chunk * tiles_per_chunk) * TILE_ROWS
        column = pl.multiple_of((chunk + index_ref[0] * HALF_CHUNKS) * LANES, LANES)
        rows = slice(step * TILE_ROWS, (step + 1) * TILE_ROWS)

        @pl.when(row < QKV_ROWS)
        def _():
            here = pl.ds(pl.multiple_of(jnp.minimum(row, QKV_ROWS - TILE_ROWS), TILE_ROWS), TILE_ROWS)
            piece_ref[rows, :] = qkv_ref[here, pl.ds(column, LANES)]

        @pl.when(row >= QKV_ROWS)
        def _():
            here = pl.ds(pl.multiple_of(jnp.maximum(row - QKV_ROWS, 0), TILE_ROWS), TILE_ROWS)
            piece_ref[rows, :] = out_ref[here, pl.ds(column, LANES)]


def weight_piece(index, qkv_t, out_weight):
    vmem = pl.BlockSpec(memory_space=pltpu.VMEM)
    return pl.pallas_call(
        piece_kernel,
        out_shape=jax.ShapeDtypeStruct((PIECE_ROWS, LANES), jnp.bfloat16),
        in_specs=[pl.BlockSpec(memory_space=pltpu.SMEM), vmem, vmem],
        out_specs=vmem,
    )(index, qkv_t, out_weight)


def norm_kernel(gain_ref, *refs):
    out_ref = refs[MATES]
    for mate in range(MATES):
        x = refs[mate][...].astype(jnp.float32)
        scale = lax.rsqrt(jnp.sum(x * x, axis=0, keepdims=True) * (1.0 / WIDTH) + epsilon)
        out_ref[:, mate * LANES:(mate + 1) * LANES] = (x * scale * gain_ref[...]).astype(jnp.bfloat16)


def normalize(gain, groups):
    vmem = pl.BlockSpec(memory_space=pltpu.VMEM)
    return pl.pallas_call(
        norm_kernel,
        out_shape=jax.ShapeDtypeStruct((WIDTH, SPAN), jnp.bfloat16),
        in_specs=[vmem] * (1 + MATES),
        out_specs=vmem,
    )(gain, *groups)


def flat(ref):
    return ref.reshape(SLAB_ROWS, LANES)


def attend_kernel(core_ref, x_ref, *refs):
    slab_refs, out_refs, scratch = refs[:2 * HEAD_STEP], refs[2 * HEAD_STEP:-3], refs[-3:]
    proj_sc, heads_sc = scratch[:2], scratch[2]
    step = pl.program_id(0)
    starts = [pl.multiple_of(core_ref[0] * HALF_WIDTH, LANES),
              pl.multiple_of((1 - core_ref[0]) * HALF_WIDTH, LANES)]
    first = lax.broadcasted_iota(jnp.int32, (WIN, LANES), 1) < WIN
    for local in range(HEAD_STEP):
        rows = pl.ds(pl.multiple_of((step * HEAD_STEP + local) * HEAD_DIM, 16), HEAD_DIM)
        projected = None
        for half in range(2):
            slab = flat(slab_refs[2 * local + half])
            bases = [chunk * HEAD_ROWS for chunk in range(HALF_CHUNKS)]
            weights = jnp.concatenate([slab[base:base + QKV_ROWS, :] for base in bases], axis=1)
            term = jnp.dot(weights, x_ref[pl.ds(starts[half], HALF_WIDTH), :], preferred_element_type=jnp.float32)
            projected = term if projected is None else projected + term
            for chunk, base in enumerate(bases):
                proj_sc[half][rows, chunk * LANES:(chunk + 1) * LANES] = slab[base + QKV_ROWS:base + HEAD_ROWS, :]
        projected = projected.astype(jnp.bfloat16)
        for mate in range(MATES):
            span = projected[:, mate * LANES:(mate + 1) * LANES]
            queries, keys, values = span[:HEAD_DIM], span[HEAD_DIM:2 * HEAD_DIM], span[2 * HEAD_DIM:]
            scores = lax.dot_general(keys, queries, (((0,), (0,)), ((), ())), preferred_element_type=jnp.float32)
            scores = jnp.where(first, scores[:WIN], scores[WIN:]) * HEAD_DIM ** (-0.5)
            scores = jnp.exp(scores - jnp.max(scores, axis=0, keepdims=True))
            probs = scores / jnp.sum(scores, axis=0, keepdims=True)
            zero = jnp.zeros_like(probs)
            probs = jnp.concatenate([jnp.where(first, probs, zero), jnp.where(first, zero, probs)], axis=0)
            out = jnp.dot(values, probs.astype(jnp.bfloat16), preferred_element_type=jnp.float32)
            heads_sc[rows, mate * LANES:(mate + 1) * LANES] = out.astype(jnp.bfloat16)

    @pl.when(step == pl.num_programs(0) - 1)
    def _():
        for half in range(2):
            partial = lax.dot_general(proj_sc[half][...], heads_sc[...], (((0,), (0,)), ((), ())),
                                      preferred_element_type=jnp.float32)
            for mate in range(MATES):
                piece = partial[:, mate * LANES:(mate + 1) * LANES]
                out_refs[mate][pl.ds(starts[half], HALF_WIDTH), :] = piece.astype(out_refs[mate].dtype)


def attend(core, x, own, other):
    whole = pl.BlockSpec((WIDTH, LANES), lambda i: (0, 0))
    slabs, specs = [], []
    for local in range(HEAD_STEP):
        for half in (own, other):
            slabs.append(half)
            specs.append(pl.BlockSpec((PIECES, None, PIECE_ROWS, LANES),
                                      lambda i, local=local: (0, HEAD_STEP * i + local, 0, 0)))
    return pl.pallas_call(
        attend_kernel,
        grid=(HEADS_HERE // HEAD_STEP,),
        out_shape=[jax.ShapeDtypeStruct((WIDTH, LANES), jnp.float32)]
        + [jax.ShapeDtypeStruct((WIDTH, LANES), jnp.bfloat16)] * (MATES - 1),
        in_specs=[pl.BlockSpec(memory_space=pltpu.SMEM), pl.BlockSpec((WIDTH, SPAN), lambda i: (0, 0))] + specs,
        out_specs=[whole] * MATES,
        scratch_shapes=[pltpu.VMEM((HEADS_HERE * HEAD_DIM, HALF_WIDTH), jnp.bfloat16)] * 2
        + [pltpu.VMEM((HEADS_HERE * HEAD_DIM, SPAN), jnp.bfloat16)],
        compiler_params=pltpu.CompilerParams(vmem_limit_bytes=24 << 20),
    )(core, x, *slabs)


def trade(value, axes):
    count = 2 ** len(axes)
    return lax.ppermute(value, axes, [(i, count - 1 - i) for i in range(count)])


def exchange(values):
    across, along, both = values
    return trade(across, ("xb",)), trade(along, ("zp",)), trade(both, ("xb", "zp"))


def body(patches, norm_gain, qkv_weight, out_weight, window_plan):
    index = lax.axis_index
    core = index("c")
    home = ((index("xa") * 2 + index("xb")) * 8 + index("y")) * 2 + core
    spot = index("zh") * 2 + index("zp")
    piece = weight_piece(jnp.stack([core, index("y")]).astype(jnp.int32), qkv_weight.T, out_weight)
    column = lax.all_gather(piece, "zh", axis=0, tiled=False).reshape(HEADS_HERE, 2, PIECE_ROWS, LANES)
    chosen = lax.dynamic_index_in_dim(column, index("xb"), 1, keepdims=False)
    own = lax.all_gather(chosen.reshape(HEADS_HERE * PIECE_ROWS, LANES), "y", axis=0, tiled=True)

    share = patches.shape[1] // WIN
    pairs = patches.reshape(16, 2, share, WIN).transpose(0, 2, 1, 3).reshape(16, share, LANES)
    mine = lax.all_to_all(pairs, ("zh", "zp"), 0, 0, tiled=True).reshape(WIDTH, LANES)
    normed = normalize(norm_gain.reshape(WIDTH, 1), (mine,) + exchange((mine, mine, mine)))
    own, normed = lax.optimization_barrier((own, normed))
    other = lax.ppermute(own, "c", [(0, 1), (1, 0)])
    shape = (PIECES, HEADS_HERE, PIECE_ROWS, LANES)
    kept, *sent = attend(core.reshape(1).astype(jnp.int32), normed, own.reshape(shape), other.reshape(shape))
    total = mine.astype(jnp.float32) + kept
    for part in exchange(sent):
        total = total + part.astype(jnp.float32)
    live = lax.dynamic_slice(window_plan, (home, spot * 2), (1, 2))[0] >= 0
    total = jnp.where(jnp.repeat(live, WIN)[None, :], total, 0.0)
    done = total.astype(jnp.bfloat16).reshape(16, share, LANES)
    back = lax.all_to_all(done, ("zh", "zp"), 0, 0, tiled=True)
    return back.reshape(16, share, 2, WIN).transpose(0, 2, 1, 3).reshape(32, share * WIN)


def solution(mesh):
    grid = Mesh(mesh.devices.reshape(2, 2, 8, 2, 8, 2), ("xa", "xb", "y", "c", "zh", "zp"))
    home, feature = ("xa", "xb", "y", "c"), ("zh", "zp")
    return jax.shard_map(
        body,
        mesh=grid,
        in_specs=(P(home, feature), P(), P(None, feature), P(feature, None), P()),
        out_specs=P(home, feature),
        check_vma=False,
    )
```

```python
import jax
import jax.numpy as jnp
from jax import lax
from jax.experimental import pallas as pl
from jax.experimental.pallas import tpu as pltpu
from jax.sharding import Mesh, PartitionSpec as P


HEAD_DIM = 80
WIN = 64
WIDTH = 1280
LANES = 128
HALF_WIDTH = WIDTH // 2
PARTS = 4
HALVES = 2
HEADS_HERE = 8
HEAD_STEP = 2
MATES = 2
SPAN = MATES * LANES
epsilon = 1e-06


def piece_kernel(place_ref, qkv_ref, out_ref, piece_ref):
    @pl.when(place_ref[0] < PARTS - 1)
    def _():
        piece_ref[...] = qkv_ref[...]

    @pl.when(place_ref[0] == PARTS - 1)
    def _():
        piece_ref[...] = out_ref[...]


def weight_piece(place, qkv_t, out_weight):
    block = (HEAD_DIM, HALF_WIDTH)
    return pl.pallas_call(
        piece_kernel,
        grid_spec=pltpu.PrefetchScalarGridSpec(
            num_scalar_prefetch=1,
            grid=(1,),
            in_specs=[
                pl.BlockSpec(block, lambda i, place: (jnp.minimum(place[0], PARTS - 2), place[1])),
                pl.BlockSpec(block, lambda i, place: (0, place[1])),
            ],
            out_specs=pl.BlockSpec(block, lambda i, place: (0, 0)),
        ),
        out_shape=jax.ShapeDtypeStruct(block, jnp.bfloat16),
        compiler_params=pltpu.CompilerParams(vmem_limit_bytes=4 << 20),
    )(place, qkv_t, out_weight)


def norm_kernel(gain_ref, *refs):
    out_ref = refs[MATES]
    for mate in range(MATES):
        x = refs[mate][...].astype(jnp.float32)
        scale = lax.rsqrt(jnp.sum(x * x, axis=0, keepdims=True) * (1.0 / WIDTH) + epsilon)
        out_ref[:, mate * LANES:(mate + 1) * LANES] = (x * scale * gain_ref[...]).astype(jnp.bfloat16)


def normalize(gain, groups):
    vmem = pl.BlockSpec(memory_space=pltpu.VMEM)
    return pl.pallas_call(
        norm_kernel,
        out_shape=jax.ShapeDtypeStruct((WIDTH, SPAN), jnp.bfloat16),
        in_specs=[vmem] * (1 + MATES),
        out_specs=vmem,
        compiler_params=pltpu.CompilerParams(vmem_limit_bytes=16 << 20),
    )(gain, *groups)


def attend_kernel(x_ref, *refs):
    slab_refs, out_refs, sum_sc = refs[:HEAD_STEP], refs[HEAD_STEP:-1], refs[-1]
    step = pl.program_id(0)
    first = lax.broadcasted_iota(jnp.int32, (WIN, LANES), 1) < WIN
    x = x_ref[...]
    heads, folds = [], []
    for slab in slab_refs:
        parts = [jnp.concatenate([slab[part, half] for half in range(HALVES)], axis=1) for part in range(PARTS)]
        projected = jnp.dot(jnp.concatenate(parts[:PARTS - 1], axis=0), x, preferred_element_type=jnp.float32)
        projected = projected.astype(jnp.bfloat16)
        outs = []
        for mate in range(MATES):
            span = projected[:, mate * LANES:(mate + 1) * LANES]
            queries, keys, values = span[:HEAD_DIM], span[HEAD_DIM:2 * HEAD_DIM], span[2 * HEAD_DIM:]
            scores = lax.dot_general(keys, queries, (((0,), (0,)), ((), ())), preferred_element_type=jnp.float32)
            scores = jnp.where(first, scores[:WIN], scores[WIN:]) * HEAD_DIM ** (-0.5)
            scores = jnp.exp(scores - jnp.max(scores, axis=0, keepdims=True))
            probs = scores / jnp.sum(scores, axis=0, keepdims=True)
            zero = jnp.zeros_like(probs)
            probs = jnp.concatenate([jnp.where(first, probs, zero), jnp.where(first, zero, probs)], axis=0)
            outs.append(jnp.dot(values, probs.astype(jnp.bfloat16), preferred_element_type=jnp.float32))
        heads.append(jnp.concatenate(outs, axis=1).astype(jnp.bfloat16))
        folds.append(parts[PARTS - 1])
    partial = lax.dot_general(jnp.concatenate(folds, axis=0), jnp.concatenate(heads, axis=0),
                              (((0,), (0,)), ((), ())), preferred_element_type=jnp.float32)

    @pl.when(step == 0)
    def _():
        sum_sc[...] = partial

    @pl.when(step > 0)
    def _():
        sum_sc[...] += partial

    @pl.when(step == pl.num_programs(0) - 1)
    def _():
        for mate in range(MATES):
            out_refs[mate][...] = sum_sc[:, mate * LANES:(mate + 1) * LANES].astype(out_refs[mate].dtype)


def attend(x, slabs):
    whole = pl.BlockSpec((WIDTH, LANES), lambda i: (0, 0))
    specs = [
        pl.BlockSpec((PARTS, HALVES, None, HEAD_DIM, HALF_WIDTH),
                     lambda i, local=local: (0, 0, HEAD_STEP * i + local, 0, 0))
        for local in range(HEAD_STEP)
    ]
    return pl.pallas_call(
        attend_kernel,
        grid=(HEADS_HERE // HEAD_STEP,),
        out_shape=[jax.ShapeDtypeStruct((WIDTH, LANES), jnp.float32),
                   jax.ShapeDtypeStruct((WIDTH, LANES), jnp.bfloat16)],
        in_specs=[pl.BlockSpec((WIDTH, SPAN), lambda i: (0, 0))] + specs,
        out_specs=[whole] * MATES,
        scratch_shapes=[pltpu.VMEM((WIDTH, SPAN), jnp.float32)],
        compiler_params=pltpu.CompilerParams(vmem_limit_bytes=58 << 20),
    )(x, *([slabs] * HEAD_STEP))


def trade(value):
    return lax.ppermute(value, "zp", [(0, 1), (1, 0)])


def body(patches, norm_gain, qkv_weight, out_weight, window_plan):
    index = lax.axis_index
    home = (index("x") * 8 + index("y")) * 2 + index("c")
    spot = index("zh") * 2 + index("zp")
    place = jnp.stack([index("x"), index("c")]).astype(jnp.int32)
    piece = weight_piece(place, qkv_weight.T, out_weight)
    column = lax.all_gather(piece, "zh", axis=0, tiled=True)
    slabs = lax.all_gather(column, ("x", "c"), axis=0, tiled=True)

    share = patches.shape[1] // WIN
    pairs = patches.reshape(16, 2, share, WIN).transpose(0, 2, 1, 3).reshape(16, share, LANES)
    mine = lax.all_to_all(pairs, ("zh", "zp"), 0, 0, tiled=True).reshape(WIDTH, LANES)
    normed = normalize(norm_gain.reshape(WIDTH, 1), (mine, trade(mine)))
    slabs, normed = lax.optimization_barrier((slabs, normed))
    kept, sent = attend(normed, slabs.reshape(PARTS, HALVES, HEADS_HERE, HEAD_DIM, HALF_WIDTH))
    total = mine.astype(jnp.float32) + kept + trade(sent).astype(jnp.float32)
    live = lax.dynamic_slice(window_plan, (home, spot * 2), (1, 2))[0] >= 0
    total = jnp.where(jnp.repeat(live, WIN)[None, :], total, 0.0)
    done = total.astype(jnp.bfloat16).reshape(16, share, LANES)
    back = lax.all_to_all(done, ("zh", "zp"), 0, 0, tiled=True)
    return back.reshape(16, share, 2, WIN).transpose(0, 2, 1, 3).reshape(32, share * WIN)


def solution(mesh):
    grid = Mesh(mesh.devices.reshape(4, 8, 2, 8, 2), ("x", "y", "c", "zh", "zp"))
    home, feature = ("x", "y", "c"), ("zh", "zp")
    return jax.shard_map(
        body,
        mesh=grid,
        in_specs=(P(home, feature), P(), P(None, feature), P(feature, None), P()),
        out_specs=P(home, feature),
        check_vma=False,
    )
```

```python
import jax
import jax.numpy as jnp
from jax import lax
from jax.experimental import pallas as pl
from jax.experimental.pallas import tpu as pltpu
from jax.sharding import Mesh, PartitionSpec as P


HEAD_DIM = 80
WIN = 64
WIDTH = 1280
LANES = 128
HALF_WIDTH = WIDTH // 2
PARTS = 4
HALVES = 2
HEADS_HERE = 8
HEAD_STEP = 8
MATES = 2
SPAN = MATES * LANES
epsilon = 1e-06


def piece_kernel(place_ref, qkv_ref, out_ref, piece_ref):
    @pl.when(place_ref[0] < PARTS - 1)
    def _():
        piece_ref[...] = qkv_ref[...]

    @pl.when(place_ref[0] == PARTS - 1)
    def _():
        piece_ref[...] = out_ref[...]


def weight_piece(place, qkv_t, out_weight):
    block = (HEAD_DIM, HALF_WIDTH)
    return pl.pallas_call(
        piece_kernel,
        grid_spec=pltpu.PrefetchScalarGridSpec(
            num_scalar_prefetch=1,
            grid=(1,),
            in_specs=[
                pl.BlockSpec(block, lambda i, place: (jnp.minimum(place[0], PARTS - 2), place[1])),
                pl.BlockSpec(block, lambda i, place: (0, place[1])),
            ],
            out_specs=pl.BlockSpec(block, lambda i, place: (0, 0)),
        ),
        out_shape=jax.ShapeDtypeStruct(block, jnp.bfloat16),
        compiler_params=pltpu.CompilerParams(vmem_limit_bytes=60 << 20),
    )(place, qkv_t, out_weight)


def norm_kernel(gain_ref, *refs):
    out_ref = refs[MATES]
    for mate in range(MATES):
        x = refs[mate][...].astype(jnp.float32)
        scale = lax.rsqrt(jnp.sum(x * x, axis=0, keepdims=True) * (1.0 / WIDTH) + epsilon)
        out_ref[:, mate * LANES:(mate + 1) * LANES] = (x * scale * gain_ref[...]).astype(jnp.bfloat16)


def normalize(gain, groups):
    vmem = pl.BlockSpec(memory_space=pltpu.VMEM)
    return pl.pallas_call(
        norm_kernel,
        out_shape=jax.ShapeDtypeStruct((WIDTH, SPAN), jnp.bfloat16),
        in_specs=[vmem] * (1 + MATES),
        out_specs=vmem,
        compiler_params=pltpu.CompilerParams(vmem_limit_bytes=16 << 20),
    )(gain, *groups)


def attend_kernel(x_ref, *refs):
    slab_refs, out_refs, sum_sc = refs[:HEAD_STEP], refs[HEAD_STEP:-1], refs[-1]
    step = pl.program_id(0)
    first = lax.broadcasted_iota(jnp.int32, (WIN, LANES), 1) < WIN

    def rows(slab, part):
        return jnp.concatenate([slab[part, half] for half in range(HALVES)], axis=1)

    weights = jnp.concatenate([rows(slab, part) for slab in slab_refs for part in range(PARTS - 1)], axis=0)
    projected = jnp.dot(weights, x_ref[...], preferred_element_type=jnp.float32).astype(jnp.bfloat16)
    spans = []
    for local in range(HEAD_STEP):
        base = local * (PARTS - 1) * HEAD_DIM
        for mate in range(MATES):
            lanes = slice(mate * LANES, (mate + 1) * LANES)
            spans.append([projected[base + part * HEAD_DIM:base + (part + 1) * HEAD_DIM, lanes]
                          for part in range(PARTS - 1)])
    scores = [lax.dot_general(keys, queries, (((0,), (0,)), ((), ())), preferred_element_type=jnp.float32)
              for queries, keys, _ in spans]
    scores = [jnp.where(first, score[:WIN], score[WIN:]) * HEAD_DIM ** (-0.5) for score in scores]
    scores = [jnp.exp(score - jnp.max(score, axis=0, keepdims=True)) for score in scores]
    probs = [score / jnp.sum(score, axis=0, keepdims=True) for score in scores]
    probs = [jnp.concatenate([jnp.where(first, prob, 0.0), jnp.where(first, 0.0, prob)], axis=0).astype(jnp.bfloat16)
             for prob in probs]
    outs = [jnp.dot(values, prob, preferred_element_type=jnp.float32).astype(jnp.bfloat16)
            for (_, _, values), prob in zip(spans, probs)]
    heads = jnp.concatenate([jnp.concatenate(outs[local * MATES:(local + 1) * MATES], axis=1)
                             for local in range(HEAD_STEP)], axis=0)
    folds = jnp.concatenate([rows(slab, PARTS - 1) for slab in slab_refs], axis=0)
    partial = lax.dot_general(heads, folds, (((0,), (0,)), ((), ())), preferred_element_type=jnp.float32)


    @pl.when(step == pl.num_programs(0) - 1)
    def _():
        for mate in range(MATES):
            lanes = slice(mate * LANES, (mate + 1) * LANES)
            out_refs[mate][...] = partial[lanes, :].T.astype(out_refs[mate].dtype)


def attend(x, slabs):
    whole = pl.BlockSpec((WIDTH, LANES), lambda i: (0, 0))
    specs = [
        pl.BlockSpec((PARTS, HALVES, None, HEAD_DIM, HALF_WIDTH),
                     lambda i, local=local: (0, 0, HEAD_STEP * i + local, 0, 0))
        for local in range(HEAD_STEP)
    ]
    return pl.pallas_call(
        attend_kernel,
        grid=(HEADS_HERE // HEAD_STEP,),
        out_shape=[jax.ShapeDtypeStruct((WIDTH, LANES), jnp.float32),
                   jax.ShapeDtypeStruct((WIDTH, LANES), jnp.bfloat16)],
        in_specs=[pl.BlockSpec((WIDTH, SPAN), lambda i: (0, 0))] + specs,
        out_specs=[whole] * MATES,
        scratch_shapes=[pltpu.VMEM((SPAN, WIDTH), jnp.float32)],
        compiler_params=pltpu.CompilerParams(vmem_limit_bytes=58 << 20),
    )(x, *([slabs] * HEAD_STEP))


def trade(value):
    return lax.ppermute(value, "zp", [(0, 1), (1, 0)])


def body(patches, norm_gain, qkv_weight, out_weight, window_plan):
    index = lax.axis_index
    home = (index("x") * 8 + index("y")) * 2 + index("c")
    spot = index("zh") * 2 + index("zp")
    place = jnp.stack([index("x"), index("c")]).astype(jnp.int32)
    piece = weight_piece(place, qkv_weight.T, out_weight)
    column = lax.all_gather(piece, "zh", axis=0, tiled=True)
    slabs = lax.all_gather(column, ("x", "c"), axis=0, tiled=True)

    share = patches.shape[1] // WIN
    pairs = patches.reshape(16, 2, share, WIN).transpose(0, 2, 1, 3).reshape(16, share, LANES)
    mine = lax.all_to_all(pairs, ("zh", "zp"), 0, 0, tiled=True).reshape(WIDTH, LANES)
    normed = normalize(norm_gain.reshape(WIDTH, 1), (mine, trade(mine)))
    slabs, normed = lax.optimization_barrier((slabs, normed))
    kept, sent = attend(normed, slabs.reshape(PARTS, HALVES, HEADS_HERE, HEAD_DIM, HALF_WIDTH))
    total = mine.astype(jnp.float32) + kept + trade(sent).astype(jnp.float32)
    live = lax.dynamic_slice(window_plan, (home, spot * 2), (1, 2))[0] >= 0
    total = jnp.where(jnp.repeat(live, WIN)[None, :], total, 0.0)
    done = total.astype(jnp.bfloat16).reshape(16, share, LANES)
    back = lax.all_to_all(done, ("zh", "zp"), 0, 0, tiled=True)
    return back.reshape(16, share, 2, WIN).transpose(0, 2, 1, 3).reshape(32, share * WIN)


def solution(mesh):
    grid = Mesh(mesh.devices.reshape(4, 8, 2, 8, 2), ("x", "y", "c", "zh", "zp"))
    home, feature = ("x", "y", "c"), ("zh", "zp")
    return jax.shard_map(
        body,
        mesh=grid,
        in_specs=(P(home, feature), P(), P(None, feature), P(feature, None), P()),
        out_specs=P(home, feature),
        check_vma=False,
    )
```

```python
import jax
import jax.numpy as jnp
from jax import lax
from jax.experimental import pallas as pl
from jax.experimental.pallas import tpu as pltpu
from jax.sharding import Mesh, PartitionSpec as P


HEAD_DIM = 80
WIN = 64
WIDTH = 1280
LANES = 128
HALF_WIDTH = WIDTH // 2
PARTS = 4
HALVES = 2
HEADS_HERE = 8
HEAD_STEP = HEADS_HERE
MATES = 2
BLOCKS = PARTS * HALVES
SPAN = MATES * LANES
epsilon = 1e-06


def piece_kernel(place_ref, qkv_ref, out_ref, piece_ref):
    @pl.when(place_ref[0] < PARTS - 1)
    def _():
        piece_ref[...] = qkv_ref[...]

    @pl.when(place_ref[0] == PARTS - 1)
    def _():
        piece_ref[...] = out_ref[...]


def weight_piece(place, qkv_t, out_weight):
    block = (HEAD_DIM, HALF_WIDTH)
    return pl.pallas_call(
        piece_kernel,
        grid_spec=pltpu.PrefetchScalarGridSpec(
            num_scalar_prefetch=1,
            grid=(1,),
            in_specs=[
                pl.BlockSpec(block, lambda i, place: (jnp.minimum(place[0], PARTS - 2), place[1])),
                pl.BlockSpec(block, lambda i, place: (0, place[1])),
            ],
            out_specs=pl.BlockSpec(block, lambda i, place: (0, 0)),
        ),
        out_shape=jax.ShapeDtypeStruct(block, jnp.bfloat16),
        compiler_params=pltpu.CompilerParams(vmem_limit_bytes=60 << 20),
    )(place, qkv_t, out_weight)


def norm_kernel(gain_ref, *refs):
    out_ref = refs[MATES]
    for mate in range(MATES):
        x = refs[mate][...].astype(jnp.float32)
        scale = lax.rsqrt(jnp.sum(x * x, axis=0, keepdims=True) * (1.0 / WIDTH) + epsilon)
        out_ref[:, mate * LANES:(mate + 1) * LANES] = (x * scale * gain_ref[...]).astype(jnp.bfloat16)


def normalize(gain, groups):
    vmem = pl.BlockSpec(memory_space=pltpu.VMEM)
    return pl.pallas_call(
        norm_kernel,
        out_shape=jax.ShapeDtypeStruct((WIDTH, SPAN), jnp.bfloat16),
        in_specs=[vmem] * (1 + MATES),
        out_specs=vmem,
        compiler_params=pltpu.CompilerParams(vmem_limit_bytes=16 << 20),
    )(gain, *groups)


def attend_kernel(place_ref, x_ref, *refs):
    block_refs, out_refs, (slabs, sems) = refs[:BLOCKS], refs[BLOCKS:-2], refs[-2:]
    first = lax.broadcasted_iota(jnp.int32, (WIN, LANES), 1) < WIN
    copies = []
    for number, block in enumerate(block_refs):
        part = (place_ref[0] + PARTS - number // HALVES) % PARTS
        half = (place_ref[1] + number) % HALVES
        copies.append(pltpu.make_async_copy(block, slabs.at[part, half], sems.at[number]))
    for copy in copies:
        copy.start()
    for copy in copies:
        copy.wait()
    slab_refs = [slabs.at[:, :, pl.ds(head * HEAD_DIM, HEAD_DIM), :] for head in range(HEADS_HERE)]

    def rows(slab, part):
        return jnp.concatenate([slab[part, half] for half in range(HALVES)], axis=1)

    weights = jnp.concatenate([rows(slab, part) for slab in slab_refs for part in range(PARTS - 1)], axis=0)
    projected = jnp.dot(weights, x_ref[...], preferred_element_type=jnp.float32).astype(jnp.bfloat16)
    spans = []
    for local in range(HEAD_STEP):
        base = local * (PARTS - 1) * HEAD_DIM
        for mate in range(MATES):
            lanes = slice(mate * LANES, (mate + 1) * LANES)
            spans.append([projected[base + part * HEAD_DIM:base + (part + 1) * HEAD_DIM, lanes]
                          for part in range(PARTS - 1)])
    scores = [lax.dot_general(keys, queries, (((0,), (0,)), ((), ())), preferred_element_type=jnp.float32)
              for queries, keys, _ in spans]
    scores = [jnp.where(first, score[:WIN], score[WIN:]) * HEAD_DIM ** (-0.5) for score in scores]
    scores = [jnp.exp(score - jnp.max(score, axis=0, keepdims=True)) for score in scores]
    probs = [score / jnp.sum(score, axis=0, keepdims=True) for score in scores]
    probs = [jnp.concatenate([jnp.where(first, prob, 0.0), jnp.where(first, 0.0, prob)], axis=0).astype(jnp.bfloat16)
             for prob in probs]
    outs = [jnp.dot(values, prob, preferred_element_type=jnp.float32).astype(jnp.bfloat16)
            for (_, _, values), prob in zip(spans, probs)]
    heads = jnp.concatenate([jnp.concatenate(outs[local * MATES:(local + 1) * MATES], axis=1)
                             for local in range(HEAD_STEP)], axis=0)
    folds = jnp.concatenate([rows(slab, PARTS - 1) for slab in slab_refs], axis=0)
    partial = lax.dot_general(heads, folds, (((0,), (0,)), ((), ())), preferred_element_type=jnp.float32)


    for mate in range(MATES):
        lanes = slice(mate * LANES, (mate + 1) * LANES)
        out_refs[mate][...] = partial[lanes, :].T.astype(out_refs[mate].dtype)


def attend(place, x, blocks):
    vmem = pl.BlockSpec(memory_space=pltpu.VMEM)
    return pl.pallas_call(
        attend_kernel,
        out_shape=[jax.ShapeDtypeStruct((WIDTH, LANES), jnp.float32),
                   jax.ShapeDtypeStruct((WIDTH, LANES), jnp.bfloat16)],
        in_specs=[pl.BlockSpec(memory_space=pltpu.SMEM), vmem] + [pl.BlockSpec(memory_space=pl.ANY)] * BLOCKS,
        out_specs=[vmem] * MATES,
        scratch_shapes=[pltpu.VMEM((PARTS, HALVES, HEADS_HERE * HEAD_DIM, HALF_WIDTH), jnp.bfloat16),
                        pltpu.SemaphoreType.DMA((BLOCKS,))],
        compiler_params=pltpu.CompilerParams(vmem_limit_bytes=56 << 20),
    )(place, x, *blocks)


def trade(value):
    return lax.ppermute(value, "zp", [(0, 1), (1, 0)])


def body(patches, norm_gain, qkv_weight, out_weight, window_plan):
    index = lax.axis_index
    home = (index("x") * 8 + index("y")) * 2 + index("c")
    spot = index("zh") * 2 + index("zp")
    place = jnp.stack([index("x"), index("c")]).astype(jnp.int32)
    piece = weight_piece(place, qkv_weight.T, out_weight)
    column = lax.all_gather(piece, "zh", axis=0, tiled=True)
    arrived = [column] + [lax.ppermute(column, "x", [(i, (i + step) % PARTS) for i in range(PARTS)])
                          for step in range(1, PARTS)]

    share = patches.shape[1] // WIN
    pairs = patches.reshape(16, 2, share, WIN).transpose(0, 2, 1, 3).reshape(16, share, LANES)
    mine = lax.all_to_all(pairs, ("zh", "zp"), 0, 0, tiled=True).reshape(WIDTH, LANES)
    normed = normalize(norm_gain.reshape(WIDTH, 1), (mine, trade(mine)))
    blocks = []
    for block in arrived:
        blocks += [block, lax.ppermute(block, "c", [(0, 1), (1, 0)])]
    kept, sent = attend(place, normed, blocks)
    total = mine.astype(jnp.float32) + kept + trade(sent).astype(jnp.float32)
    live = lax.dynamic_slice(window_plan, (home, spot * 2), (1, 2))[0] >= 0
    total = jnp.where(jnp.repeat(live, WIN)[None, :], total, 0.0)
    done = total.astype(jnp.bfloat16).reshape(16, share, LANES)
    back = lax.all_to_all(done, ("zh", "zp"), 0, 0, tiled=True)
    return back.reshape(16, share, 2, WIN).transpose(0, 2, 1, 3).reshape(32, share * WIN)


def solution(mesh):
    grid = Mesh(mesh.devices.reshape(4, 8, 2, 8, 2), ("x", "y", "c", "zh", "zp"))
    home, feature = ("x", "y", "c"), ("zh", "zp")
    return jax.shard_map(
        body,
        mesh=grid,
        in_specs=(P(home, feature), P(), P(None, feature), P(feature, None), P()),
        out_specs=P(home, feature),
        check_vma=False,
    )
```
